32 devices in a mesh: seq: 4 (over y, x), resp: 8 (over z, core).
Axes of the slice: x: 2, y: 2, z: 4, core: 2. Of those that a mesh axis runs over, the one named last changes fastest.
Arguments:
- queries: bfloat16 [8, 2048, 1024], P('resp', 'seq'), may hold values from -1.796875 to 1.796875
- keys: bfloat16 [8, 2048, 1024], P('resp', 'seq'), may hold values from -1.796875 to 1.796875
- values: bfloat16 [8, 2048, 1024], P('resp', 'seq'), may hold values from -6 to 6
- grad_out: bfloat16 [8, 2048, 1024], P('resp', 'seq'), may hold values from -6 to 6
- lengths: int32 [7], replicated, may hold values from 2 to 4
Outputs:
- attended: bfloat16 [8, 2048, 1024], P('resp', 'seq')
- grad_queries: bfloat16 [8, 2048, 1024], P('resp', 'seq')
- grad_keys: bfloat16 [8, 2048, 1024], P('resp', 'seq')
- grad_values: bfloat16 [8, 2048, 1024], P('resp', 'seq')
The draws below stay inside these ranges and needn't reach their ends.
All inputs are finite; a program needn't handle non-finite values.
Results may differ from the reference program's by a relative error of at most 0.005.
Values sent between devices are 32-bit elements; how exact they have to be, the bound alone decides.
No kernel may reach another device: no remote copies, remote signals or barrier semaphores. Data moves between devices by JAX's collectives and lax.ppermute only.
A program may use at most 128 MiB of HBM per device.

```python
import math
import jax
import jax.numpy as jnp
from jax import lax

HEADS = 8
HEAD = 128
BLOCK = 512
ROW_TOKENS = 2048
ROWS = 8
RESP_BLOCKS = 4


def touch_ends(drawn, rng, low, top_value):
    spot = [jax.random.randint(jax.random.fold_in(rng, axis), (), 0, length) for axis, length in enumerate(drawn.shape)]
    longest = drawn.shape.index(max(drawn.shape))
    neighbour = spot[:longest] + [(spot[longest] + 1) % drawn.shape[longest]] + spot[longest + 1:]
    return drawn.at[tuple(spot)].set(low).at[tuple(neighbour)].set(top_value)


def steps_of(rng, extent, pieces, low, largest):
    def one(position, parts):
        steps = jax.random.uniform(jax.random.fold_in(jax.random.fold_in(rng, 6), position), (parts,), jnp.float32, low / len(pieces), largest / len(pieces))
        return jnp.repeat(jnp.exp(steps), extent[position] // parts).reshape((-1,) + (1,) * (len(extent) - position - 1))

    level = one(*pieces[0])
    for cut in pieces[1:]:
        level = level * one(*cut)
    return level


def scatter_about(own_key, shape, scale, reach, pieces=(), held_as=jnp.bfloat16):
    entries = scale * jax.random.normal(own_key, shape, jnp.float32)
    if pieces:
        entries = entries * steps_of(own_key, shape, pieces, -0.22, 0.18)
    return jnp.clip(entries, -reach, reach).astype(held_as)


def setup_inputs(seed: int = 0) -> dict:
    key_of = jax.random.split(jax.random.key(seed), 6)
    return {
        "queries": scatter_about(key_of[0], (ROWS, ROW_TOKENS, HEADS * HEAD), 0.3, 1.796875, ((0, 8), (1, 4))),
        "keys": scatter_about(key_of[1], (ROWS, ROW_TOKENS, HEADS * HEAD), 0.3, 1.796875, ((0, 8), (1, 4))),
        "values": scatter_about(key_of[2], (ROWS, ROW_TOKENS, HEADS * HEAD), 1.0, 6.0, ((0, 8), (1, 4))),
        "grad_out": scatter_about(key_of[3], (ROWS, ROW_TOKENS, HEADS * HEAD), 1.0, 6.0, ((0, 8), (1, 4))),
        "lengths": touch_ends(jax.random.randint(key_of[4], (ROWS - 1,), RESP_BLOCKS // 2, RESP_BLOCKS + 1), jax.random.fold_in(key_of[4], 1), RESP_BLOCKS // 2, RESP_BLOCKS).astype(jnp.int32),
    }


def lower_round(array):
    narrow = lax.optimization_barrier(array.astype(jnp.bfloat16))
    return narrow.astype(jnp.float32)

def block_pass(query_block, key_block, value_block, grad_block, forward_state, backward_state, factor):
    block_rows = query_block.shape[0]
    causal = (jnp.arange(block_rows)[:, None] >= jnp.arange(block_rows)[None, :])[None]
    query_wide = query_block.astype(jnp.float32)
    key_wide = key_block.astype(jnp.float32)
    value_wide = value_block.astype(jnp.float32)
    grad_wide = grad_block.astype(jnp.float32)
    attend = lower_round(jnp.where(causal, jnp.einsum('thd,shd->hts', query_wide, key_wide) * factor, 0.0))
    pushed = lower_round(jnp.where(causal, jnp.einsum('thd,shd->hts', grad_wide, value_wide) * factor, 0.0))
    forward_low = lower_round(forward_state)
    backward_low = lower_round(backward_state)
    attended = jnp.einsum('hts,shd->thd', attend, value_wide) + factor * jnp.einsum('thi,hij->thj', query_wide, forward_low)
    grad_query = jnp.einsum('hts,shi->thi', pushed, key_wide) + factor * jnp.einsum('thj,hij->thi', grad_wide, forward_low)
    grad_key = jnp.einsum('hts,thi->shi', pushed, query_wide) + factor * jnp.einsum('shj,hij->shi', value_wide, backward_low)
    grad_value = jnp.einsum('hts,thi->shi', attend, grad_wide) + factor * jnp.einsum('shi,hij->shj', key_wide, backward_low)
    return (attended.astype(jnp.bfloat16), grad_query.astype(jnp.bfloat16), grad_key.astype(jnp.bfloat16), grad_value.astype(jnp.bfloat16))

def reference(queries, keys, values, grad_out, lengths):
    row_count = queries.shape[0]
    length = queries.shape[1]
    row_width = queries.shape[2]
    factor = 1.0 / math.sqrt(2.0 * length)
    limits = jnp.concatenate([jnp.array([length], dtype=jnp.int32), (lengths * BLOCK).astype(jnp.int32)])
    keep_mask = (jnp.arange(length, dtype=jnp.int32)[None, :] < limits[:, None]).astype(jnp.bfloat16)[:, :, None]
    masked = tuple(((array * keep_mask).reshape(row_count, length, HEADS, HEAD) for array in (queries, keys, values, grad_out)))

    def totals(arrays):
        query_row, key_row, value_row, grad_row = arrays
        state_kv = jnp.einsum('thi,thj->hij', key_row.astype(jnp.float32), value_row.astype(jnp.float32))
        state_qg = jnp.einsum('thi,thj->hij', query_row.astype(jnp.float32), grad_row.astype(jnp.float32))
        return (state_kv, state_qg)
    kv_rows, qg_rows = lax.map(totals, masked)
    prompt_state = kv_rows[0]
    answer_state = lax.optimization_barrier(jnp.sum(qg_rows[1:], axis=0))
    blocks = length // BLOCK

    def one_row(arrays):
        row_index = arrays[0]
        shaped = tuple((array.reshape(blocks, BLOCK, HEADS, HEAD) for array in arrays[1:]))
        kv_blocks = jnp.einsum('bthi,bthj->bhij', shaped[1].astype(jnp.float32), shaped[2].astype(jnp.float32))
        qg_blocks = jnp.einsum('bthi,bthj->bhij', shaped[0].astype(jnp.float32), shaped[3].astype(jnp.float32))
        start_state = jnp.where(row_index == 0, jnp.zeros_like(prompt_state), prompt_state)
        end_state = jnp.where(row_index == 0, answer_state, jnp.zeros_like(answer_state))
        forward = start_state[None] + jnp.cumsum(kv_blocks, axis=0) - kv_blocks
        backward = end_state[None] + (lax.optimization_barrier(jnp.sum(qg_blocks, axis=0))[None] - jnp.cumsum(qg_blocks, axis=0))
        results = lax.map(lambda items: block_pass(items[0], items[1], items[2], items[3], items[4], items[5], factor), (shaped[0], shaped[1], shaped[2], shaped[3], forward, backward))
        return tuple((result.reshape(length, row_width) for result in results))
    outputs = lax.map(one_row, (jnp.arange(row_count, dtype=jnp.int32), masked[0], masked[1], masked[2], masked[3]))
    return (outputs[0], outputs[1], outputs[2], outputs[3])
```

```python
import functools
import math

import jax
import jax.numpy as jnp
from jax import lax
from jax.experimental import pallas as pl
from jax.experimental.pallas import tpu as pltpu
from jax.sharding import PartitionSpec as P

HEADS = 8
HEAD = 128
BLOCK = 512
TILE = 256
F32 = jnp.float32
BF16 = jnp.bfloat16
AXES = ("seq", "resp")

NN = (((1,), (0,)), ((), ()))
NT = (((1,), (1,)), ((), ()))
TN = (((0,), (0,)), ((), ()))


def dot(a, b, dims):
    return lax.dot_general(a, b, dims, preferred_element_type=F32)


def kept(lengths_ref):
    row = lax.axis_index("resp")
    limit = lengths_ref[jnp.maximum(row - 1, 0)]
    return jnp.logical_or(row == 0, lax.axis_index("seq") < limit)


def state_kernel(bits, lengths_ref, q_ref, k_ref, v_ref, g_ref, *outs):
    keep = kept(lengths_ref)
    place = lax.axis_index("seq")
    row = lax.axis_index("resp")
    kv = jnp.where(keep, dot(k_ref[...], v_ref[...], TN), 0.0)
    qg = jnp.where(keep, dot(q_ref[...], g_ref[...], TN), 0.0)
    for bit in range(bits):
        late = lax.rem(lax.div(place, 2**bit), 2) == 1
        outs[bit][...] = jnp.where(late, qg, kv)
    outs[bits][...] = jnp.where(row == 0, kv, qg)


def inner_kernel(factor, q_ref, k_ref, v_ref, g_ref, att_ref, gq_ref, gk_ref, gv_ref):
    tiles = q_ref.shape[0] // TILE
    cut = [pl.ds(i * TILE, TILE) for i in range(tiles)]
    q, k, v, g = ([ref[c, :] for c in cut] for ref in (q_ref, k_ref, v_ref, g_ref))
    rows = lax.broadcasted_iota(jnp.int32, (TILE, TILE), 0)
    columns = lax.broadcasted_iota(jnp.int32, (TILE, TILE), 1)
    causal = rows >= columns
    att, gq, gk, gv = ([None] * tiles for _ in range(4))

    def add(where, at, term):
        where[at] = term if where[at] is None else where[at] + term

    for i in range(tiles):
        for j in range(i + 1):
            a = dot(q[i], k[j], NT) * factor
            p = dot(g[i], v[j], NT) * factor
            if i == j:
                a = jnp.where(causal, a, 0.0)
                p = jnp.where(causal, p, 0.0)
            a = a.astype(BF16)
            p = p.astype(BF16)
            add(att, i, dot(a, v[j], NN))
            add(gq, i, dot(p, k[j], NN))
            add(gk, j, dot(p, q[i], TN))
            add(gv, j, dot(a, g[i], TN))
    for ref, parts in ((att_ref, att), (gq_ref, gq), (gk_ref, gk), (gv_ref, gv)):
        for c, part in zip(cut, parts):
            ref[c, :] = part


def outer_kernel(n, factor, lengths_ref, *refs):
    q_ref, k_ref, v_ref, g_ref = refs[:4]
    parts = refs[4:8]
    came = refs[8 : 8 + n - 1]
    own_ref, other_ref = refs[8 + n - 1 : 8 + n + 1]
    outs = refs[8 + n + 1 :]
    keep = kept(lengths_ref)
    place = lax.axis_index("seq")
    row = lax.axis_index("resp")
    fs = jnp.zeros((HEAD, HEAD), F32)
    bs = jnp.zeros((HEAD, HEAD), F32)
    for m in range(1, n):
        earlier = lax.rem(lax.div(place, 2 ** (m.bit_length() - 1)), 2) == 1
        new = came[m - 1][...]
        fs = fs + jnp.where(earlier, new, 0.0)
        bs = bs + jnp.where(earlier, 0.0, new)
    mine = jnp.logical_and(lax.rem(row, 2) == 0, row > 0)
    shared = jnp.where(mine, own_ref[...], other_ref[...])
    fs = (fs + jnp.where(row == 0, 0.0, shared)).astype(BF16)
    bs = (bs + jnp.where(row == 0, shared, 0.0)).astype(BF16)
    terms = (
        dot(q_ref[...], fs, NN),
        dot(g_ref[...], fs, NT),
        dot(v_ref[...], bs, NT),
        dot(k_ref[...], bs, NN),
    )
    for out, part, term in zip(outs, parts, terms):
        out[...] = jnp.where(keep, part[...] + factor * term, 0.0).astype(BF16)


def split_kernel(n, a_ref, b_ref, *outs):
    place = lax.axis_index("seq")
    for m in range(n):
        at = jnp.bitwise_xor(place, m)
        outs[m][...] = a_ref[at] + b_ref[at]


def join_kernel(n, *refs):
    place = lax.axis_index("seq")
    out = refs[n]
    for m in range(n):
        out[jnp.bitwise_xor(place, m)] = refs[m][...]


def per_device(n, rows, queries, keys, values, grad_out, lengths):
    tokens = queries.shape[1]
    width = queries.shape[2]
    factor = 1.0 / math.sqrt(2.0 * tokens * n)
    bits = n.bit_length() - 1
    layers = rows // 2
    q, k, v, g = (x.reshape(tokens, width) for x in (queries, keys, values, grad_out))
    token_spec = pl.BlockSpec((tokens, HEAD), lambda h, *_: (0, h))
    state_spec = pl.BlockSpec((HEAD, HEAD), lambda h, *_: (h, 0))
    whole = pl.BlockSpec(memory_space=pltpu.VMEM)
    state_shape = jax.ShapeDtypeStruct((HEADS * HEAD, HEAD), F32)
    size = tokens * width

    def line(s, r):
        return s * rows + r

    def move(x, pairs):
        return lax.ppermute(x, AXES, pairs)

    with jax.named_scope("state"):
        *sends, share = pl.pallas_call(
            functools.partial(state_kernel, bits),
            grid_spec=pltpu.PrefetchScalarGridSpec(
                num_scalar_prefetch=1,
                grid=(HEADS,),
                in_specs=[token_spec] * 4,
                out_specs=[state_spec] * (bits + 1),
            ),
            out_shape=[state_shape] * (bits + 1),
            compiler_params=pltpu.CompilerParams(vmem_limit_bytes=16 * 2**20),
            cost_estimate=pl.CostEstimate(
                flops=4 * size * HEAD, bytes_accessed=8 * size, transcendentals=0
            ),
        )(lengths, q, k, v, g)

    with jax.named_scope("pair"):
        mate = move(share, [(line(s, r), line(s, r + 1)) for s in range(n) for r in range(2, rows, 2)])
    piece = HEADS * HEAD // n
    piece_shape = jax.ShapeDtypeStruct((piece, HEAD), F32)
    with jax.named_scope("split"):
        pieces = pl.pallas_call(
            functools.partial(split_kernel, n),
            in_specs=[whole] * 2,
            out_specs=[whole] * n,
            out_shape=[piece_shape] * n,
            compiler_params=pltpu.CompilerParams(vmem_limit_bytes=8 * 2**20),
        )(share.reshape(n, piece, HEAD), mate.reshape(n, piece, HEAD))
    total = pieces[0]
    inward = [r for r in range(rows) if r % 2 == 1 or r == 0]
    for m in range(1, n):
        with jax.named_scope(f"gather{m}"):
            total = total + move(
                pieces[m], [(line(s, r), line(s ^ m, r)) for s in range(n) for r in inward]
            )
    row = lax.axis_index("resp")
    spare = jnp.logical_and(row % 2 == 0, row > 0)
    level = jnp.where(spare, 0.0, total)
    for z in range(1, layers):
        with jax.named_scope(f"level{z}"):
            level = level + move(
                total,
                [(line(s, 2 * z + 1), line(s, 1)) for s in range(n)]
                + [(line(s, 0), line(s, 2 * z)) for s in range(n)],
            )
    outward = [r for r in range(rows) if r % 2 == 0 or r == 1]
    spread = [level]
    for m in range(1, n):
        with jax.named_scope(f"spread{m}"):
            spread.append(
                move(level, [(line(s, r), line(s ^ m, r)) for s in range(n) for r in outward])
            )
    with jax.named_scope("join"):
        own = pl.pallas_call(
            functools.partial(join_kernel, n),
            in_specs=[whole] * n,
            out_specs=whole,
            out_shape=jax.ShapeDtypeStruct((n, piece, HEAD), F32),
            compiler_params=pltpu.CompilerParams(vmem_limit_bytes=8 * 2**20),
        )(*spread).reshape(HEADS * HEAD, HEAD)
    with jax.named_scope("swap"):
        other = move(
            own,
            [(line(s, r), line(s, r + 1)) for s in range(n) for r in range(0, rows, 2)]
            + [(line(s, 1), line(s, 0)) for s in range(n)],
        )
    came = []
    for m in range(1, n):
        with jax.named_scope(f"scan{m}"):
            came.append(
                move(
                    sends[m.bit_length() - 1],
                    [(line(s, r), line(s ^ m, r)) for s in range(n) for r in range(rows)],
                )
            )
    part_shape = jax.ShapeDtypeStruct((tokens, width), F32)
    with jax.named_scope("inner"):
        parts = pl.pallas_call(
            functools.partial(inner_kernel, factor),
            grid=(HEADS,),
            in_specs=[token_spec] * 4,
            out_specs=[token_spec] * 4,
            out_shape=[part_shape] * 4,
            compiler_params=pltpu.CompilerParams(vmem_limit_bytes=20 * 2**20),
            cost_estimate=pl.CostEstimate(
                flops=9 * size * tokens, bytes_accessed=24 * size, transcendentals=0
            ),
        )(q, k, v, g)
    with jax.named_scope("outer"):
        outs = pl.pallas_call(
            functools.partial(outer_kernel, n, factor),
            grid_spec=pltpu.PrefetchScalarGridSpec(
                num_scalar_prefetch=1,
                grid=(HEADS,),
                in_specs=[token_spec] * 8 + [state_spec] * (n + 1),
                out_specs=[token_spec] * 4,
            ),
            out_shape=[jax.ShapeDtypeStruct((tokens, width), BF16)] * 4,
            compiler_params=pltpu.CompilerParams(vmem_limit_bytes=20 * 2**20),
            cost_estimate=pl.CostEstimate(
                flops=8 * size * HEAD, bytes_accessed=32 * size, transcendentals=0
            ),
        )(lengths, q, k, v, g, *parts, *came, own, other)
    return tuple(x.reshape(1, tokens, width) for x in outs)


def solution(mesh):
    spec = P("resp", "seq", None)
    return jax.shard_map(
        functools.partial(per_device, mesh.shape["seq"], mesh.shape["resp"]),
        mesh=mesh,
        in_specs=(spec, spec, spec, spec, P()),
        out_specs=(spec, spec, spec, spec),
        check_vma=False,
    )
```

```python
import functools
import math

import jax
import jax.numpy as jnp
from jax import lax
from jax.experimental import pallas as pl
from jax.experimental.pallas import tpu as pltpu
from jax.sharding import PartitionSpec as P


HEADS = 8
HEAD = 128
TILE = 256
F32 = jnp.float32
BF16 = jnp.bfloat16
AXES = ("seq", "resp")

NN = (((1,), (0,)), ((), ()))
NT = (((1,), (1,)), ((), ()))
TN = (((0,), (0,)), ((), ()))


def dot(a, b, dims):
    return lax.dot_general(a, b, dims, preferred_element_type=F32)


def kept(lengths_ref):
    row = lax.axis_index("resp")
    limit = lengths_ref[jnp.maximum(row - 1, 0)]
    return jnp.logical_or(row == 0, lax.axis_index("seq") < limit)


def state_kernel(bits, lengths_ref, q_ref, k_ref, v_ref, g_ref, *outs):
    keep = kept(lengths_ref)
    place = lax.axis_index("seq")
    row = lax.axis_index("resp")
    kv = jnp.where(keep, dot(k_ref[...], v_ref[...], TN), 0.0)
    qg = jnp.where(keep, dot(q_ref[...], g_ref[...], TN), 0.0)
    for bit in range(bits):
        late = lax.rem(lax.div(place, 2**bit), 2) == 1
        outs[bit][...] = jnp.where(late, qg, kv)
    outs[bits][...] = jnp.where(row == 0, kv, qg)


def inner_kernel(factor, q_ref, k_ref, v_ref, g_ref, att_ref, gq_ref, gk_ref, gv_ref):
    tiles = q_ref.shape[0] // TILE
    cut = [pl.ds(i * TILE, TILE) for i in range(tiles)]
    q, k, v, g = ([ref[c, :] for c in cut] for ref in (q_ref, k_ref, v_ref, g_ref))
    rows = lax.broadcasted_iota(jnp.int32, (TILE, TILE), 0)
    columns = lax.broadcasted_iota(jnp.int32, (TILE, TILE), 1)
    causal = rows >= columns
    att, gq, gk, gv = ([None] * tiles for _ in range(4))

    def add(where, at, term):
        where[at] = term if where[at] is None else where[at] + term

    for i in range(tiles):
        for j in range(i + 1):
            a = dot(q[i], k[j], NT) * factor
            p = dot(g[i], v[j], NT) * factor
            if i == j:
                a = jnp.where(causal, a, 0.0)
                p = jnp.where(causal, p, 0.0)
            a = a.astype(BF16)
            p = p.astype(BF16)
            add(att, i, dot(a, v[j], NN))
            add(gq, i, dot(p, k[j], NN))
            add(gk, j, dot(p, q[i], TN))
            add(gv, j, dot(a, g[i], TN))
    for ref, parts in ((att_ref, att), (gq_ref, gq), (gk_ref, gk), (gv_ref, gv)):
        for c, part in zip(cut, parts):
            ref[c, :] = part


def outer_kernel(n, factor, lengths_ref, *refs):
    q_ref, k_ref, v_ref, g_ref = refs[:4]
    parts = refs[4:8]
    head = pl.program_id(0)
    mine = pl.ds(pl.multiple_of(head * HEAD, HEAD), HEAD)
    came = refs[8 : 8 + n - 1]
    share_ref = refs[8 + n - 1]
    outs = refs[8 + n :]
    keep = kept(lengths_ref)
    place = lax.axis_index("seq")
    row = lax.axis_index("resp")
    fs = jnp.zeros((HEAD, HEAD), F32)
    bs = jnp.zeros((HEAD, HEAD), F32)
    for m in range(1, n):
        earlier = lax.rem(lax.div(place, 2 ** (m.bit_length() - 1)), 2) == 1
        new = came[m - 1][mine, :]
        fs = fs + jnp.where(earlier, new, 0.0)
        bs = bs + jnp.where(earlier, 0.0, new)
    shared = share_ref[mine, :]
    fs = (fs + jnp.where(row == 0, 0.0, shared)).astype(BF16)
    bs = (bs + jnp.where(row == 0, shared, 0.0)).astype(BF16)
    terms = (
        dot(q_ref[...], fs, NN),
        dot(g_ref[...], fs, NT),
        dot(v_ref[...], bs, NT),
        dot(k_ref[...], bs, NN),
    )
    for out, part, term in zip(outs, parts, terms):
        out[...] = jnp.where(keep, part[:, mine] + factor * term, 0.0).astype(BF16)


def share_kernel(n, rows, came_ref, out_ref):
    prompt = jnp.zeros(came_ref.shape[1:], F32)
    answer = jnp.zeros(came_ref.shape[1:], F32)
    for s in range(n):
        prompt = prompt + came_ref[s * rows]
        for r in range(1, rows):
            answer = answer + came_ref[s * rows + r]
    for s in range(n):
        out_ref[s * rows] = answer
        for r in range(1, rows):
            out_ref[s * rows + r] = prompt


def per_device(n, rows, queries, keys, values, grad_out, lengths):
    tokens = queries.shape[1]
    width = queries.shape[2]
    factor = 1.0 / math.sqrt(2.0 * tokens * n)
    bits = n.bit_length() - 1
    q, k, v, g = (
        pltpu.with_memory_space_constraint(x.reshape(tokens, width), pltpu.HBM)
        for x in (queries, keys, values, grad_out)
    )
    token_spec = pl.BlockSpec((tokens, HEAD), lambda h, *_: (0, h))
    state_spec = pl.BlockSpec((HEAD, HEAD), lambda h, *_: (h, 0))
    whole = pl.BlockSpec(memory_space=pltpu.VMEM)
    state_shape = jax.ShapeDtypeStruct((HEADS * HEAD, HEAD), F32)
    size = tokens * width

    def line(s, r):
        return s * rows + r

    def move(x, pairs):
        return lax.ppermute(x, AXES, pairs)

    *sends, share = pl.pallas_call(
        functools.partial(state_kernel, bits),
        grid_spec=pltpu.PrefetchScalarGridSpec(
            num_scalar_prefetch=1,
            grid=(HEADS,),
            in_specs=[token_spec] * 4,
            out_specs=[state_spec] * (bits + 1),
        ),
        out_shape=[state_shape] * (bits + 1),
        compiler_params=pltpu.CompilerParams(vmem_limit_bytes=16 * 2**20),
        cost_estimate=pl.CostEstimate(
            flops=4 * size * HEAD, bytes_accessed=8 * size, transcendentals=0
        ),
    )(lengths, q, k, v, g)

    devices = n * rows
    piece = HEADS * HEAD // devices
    share = share.reshape(devices, piece, HEAD)
    share = lax.all_to_all(share, AXES, 0, 0, tiled=True)
    share = pl.pallas_call(
        functools.partial(share_kernel, n, rows),
        in_specs=[whole],
        out_specs=whole,
        out_shape=jax.ShapeDtypeStruct(share.shape, F32),
        compiler_params=pltpu.CompilerParams(vmem_limit_bytes=8 * 2**20),
    )(share)
    share = lax.all_to_all(share, AXES, 0, 0, tiled=True)
    share = share.reshape(HEADS * HEAD, HEAD)
    came = []
    for m in range(1, n):
        came.append(
            move(
                sends[m.bit_length() - 1],
                [(line(s, r), line(s ^ m, r)) for s in range(n) for r in range(rows)],
            )
        )
    part_shape = jax.ShapeDtypeStruct((tokens, width), F32)
    parts = pl.pallas_call(
        functools.partial(inner_kernel, factor),
        grid=(HEADS,),
        in_specs=[token_spec] * 4,
        out_specs=[token_spec] * 4,
        out_shape=[part_shape] * 4,
        compiler_params=pltpu.CompilerParams(vmem_limit_bytes=20 * 2**20),
        cost_estimate=pl.CostEstimate(
            flops=9 * size * tokens, bytes_accessed=24 * size, transcendentals=0
        ),
    )(q, k, v, g)
    outs = pl.pallas_call(
        functools.partial(outer_kernel, n, factor),
        grid_spec=pltpu.PrefetchScalarGridSpec(
            num_scalar_prefetch=1,
            grid=(HEADS,),
            in_specs=[token_spec] * 4 + [whole] * (n + 4),
            out_specs=[token_spec] * 4,
        ),
        out_shape=[jax.ShapeDtypeStruct((tokens, width), BF16)] * 4,
        compiler_params=pltpu.CompilerParams(vmem_limit_bytes=20 * 2**20),
        cost_estimate=pl.CostEstimate(
            flops=8 * size * HEAD, bytes_accessed=32 * size, transcendentals=0
        ),
    )(lengths, q, k, v, g, *parts, *came, share)
    return tuple(x.reshape(1, tokens, width) for x in outs)


def solution(mesh):
    n = mesh.shape["seq"]
    spec = P("resp", "seq", None)

    def body(*args):
        return per_device(n, mesh.shape["resp"], *args)

    return jax.shard_map(
        body,
        mesh=mesh,
        in_specs=(spec, spec, spec, spec, P()),
        out_specs=(spec, spec, spec, spec),
        check_vma=False,
    )
```

```python
import functools
import math

import jax
import jax.numpy as jnp
from jax import lax
from jax.experimental import pallas as pl
from jax.experimental.pallas import tpu as pltpu
from jax.sharding import PartitionSpec as P


HEADS = 8
HEAD = 128
TILE = 256
GROUPS = 4
STATE_VMEM = 12
WRITE = 4
F32 = jnp.float32
BF16 = jnp.bfloat16
AXES = ("seq", "resp")

NN = (((1,), (0,)), ((), ()))
NT = (((1,), (1,)), ((), ()))
TN = (((0,), (0,)), ((), ()))


def dot(a, b, dims):
    return lax.dot_general(a, b, dims, preferred_element_type=F32)


def kept(lengths_ref):
    row = lax.axis_index("resp")
    limit = lengths_ref[jnp.maximum(row - 1, 0)]
    return jnp.logical_or(row == 0, lax.axis_index("seq") < limit)


def state_kernel(n, *refs):
    ins = refs[:5]
    share_refs = refs[5 : 5 + n]
    rest_refs = refs[5 + n : 5 + 2 * n]
    q_ref, k_ref, v_ref, g_ref = held = refs[5 + 2 * n : 9 + 2 * n]
    share, rest, lengths_ref, sem = refs[9 + 2 * n :]
    piece = share_refs[0].shape[0]
    counts = pltpu.make_async_copy(ins[4], lengths_ref, sem.at[4])
    counts.start()
    copies = [pltpu.make_async_copy(ins[i], held[i], sem.at[i]) for i in (1, 2, 0, 3)]
    for copy in copies:
        copy.start()
    place = lax.axis_index("seq")
    prompt = lax.axis_index("resp") == 0
    heads = [pl.ds(h * HEAD, HEAD) for h in range(HEADS)]
    counts.wait()
    keep = kept(lengths_ref)
    copies[0].wait()
    copies[1].wait()
    for h in heads:
        rest[h, :] = jnp.where(keep, dot(k_ref[:, h], v_ref[:, h], TN), 0.0)
    copies[2].wait()
    copies[3].wait()
    for h in heads:
        kv = rest[h, :]
        qg = jnp.where(keep, dot(q_ref[:, h], g_ref[:, h], TN), 0.0)
        share[h, :] = jnp.where(prompt, kv, qg)
        rest[h, :] = jnp.where(prompt, qg, kv)
    for m in range(n):
        at = pl.multiple_of(jnp.bitwise_xor(place, m) * piece, piece)
        share_refs[m][...] = share[pl.ds(at, piece), :]
        rest_refs[m][...] = rest[pl.ds(at, piece), :]


def inner_kernel(factor, first, q_ref, k_ref, v_ref, g_ref, *outs):
    tiles = q_ref.shape[0] // TILE
    cut = [pl.ds(i * TILE, TILE) for i in range(tiles)]
    rows = lax.broadcasted_iota(jnp.int32, (TILE, TILE), 0)
    columns = lax.broadcasted_iota(jnp.int32, (TILE, TILE), 1)
    causal = rows >= columns
    for h in range(outs[0].shape[1] // HEAD):
        here = pl.ds((first + h) * HEAD, HEAD)
        q, k, v, g = ([ref[c, here] for c in cut] for ref in (q_ref, k_ref, v_ref, g_ref))
        sums = [[None] * tiles for _ in range(4)]

        def add(which, at, term):
            old = sums[which][at]
            sums[which][at] = term if old is None else old + term

        for i in range(tiles):
            for j in range(i + 1):
                a = dot(q[i], k[j], NT) * factor
                p = dot(g[i], v[j], NT) * factor
                if i == j:
                    a = jnp.where(causal, a, 0.0)
                    p = jnp.where(causal, p, 0.0)
                a = a.astype(BF16)
                p = p.astype(BF16)
                add(0, i, dot(a, v[j], NN))
                add(1, i, dot(p, k[j], NN))
                add(2, j, dot(p, q[i], TN))
                add(3, j, dot(a, g[i], TN))
        for ref, parts in zip(outs, sums):
            for c, part in zip(cut, parts):
                ref[c, pl.ds(h * HEAD, HEAD)] = part


def outer_kernel(factor, groups, n, lengths_hbm, *refs):
    q_ref, k_ref, v_ref, g_ref = refs[:4]
    parts = refs[4 : 4 + 4 * groups]
    refs = refs[4 + 4 * groups :]
    share_refs, rest_refs = refs[:n], refs[n : 2 * n]
    outs = refs[2 * n : 2 * n + 4]
    buffers = refs[2 * n + 4 : 2 * n + 8]
    share, rest, lengths_ref, sem, count_sem = refs[2 * n + 8 :]
    counts = pltpu.make_async_copy(lengths_hbm, lengths_ref, count_sem)
    counts.start()
    place = lax.axis_index("seq")
    prompt = lax.axis_index("resp") == 0
    piece = share_refs[0].shape[0]
    for m in range(n):
        at = pl.multiple_of(jnp.bitwise_xor(place, m) * piece, piece)
        share[pl.ds(at, piece), :] = share_refs[m][...]
        rest[pl.ds(at, piece), :] = rest_refs[m][...]
    counts.wait()
    keep = kept(lengths_ref)
    span = HEADS // groups
    copies = []
    for head in range(HEADS):
        h = pl.ds(head * HEAD, HEAD)
        within = pl.ds(head % span * HEAD, HEAD)
        fs = jnp.where(prompt, share[h, :], rest[h, :]).astype(BF16)
        bs = jnp.where(prompt, rest[h, :], share[h, :]).astype(BF16)
        sides = ((q_ref, fs, NN), (g_ref, fs, NT), (v_ref, bs, NT), (k_ref, bs, NN))
        for which, (ref, state, dims) in enumerate(sides):
            part = parts[head // span * 4 + which][:, within]
            total = part + factor * dot(ref[:, h], state, dims)
            buffers[which][:, h] = jnp.where(keep, total, 0.0).astype(BF16)
        if head % WRITE == WRITE - 1:
            at = head // WRITE
            wide = pl.ds(at * WRITE * HEAD, WRITE * HEAD)
            for which in range(4):
                copy = pltpu.make_async_copy(
                    buffers[which].at[:, wide], outs[which].at[:, wide], sem.at[which, at]
                )
                copy.start()
                copies.append(copy)
    for copy in copies:
        copy.wait()


def step_kernel(step, total_ref, new_ref, answer_ref, total_out, answer_out):
    row = lax.axis_index("resp")
    gets = jnp.logical_and(row >= step, row < 2 * step)
    total = total_ref[...]
    new = new_ref[...]
    summed = jnp.where(row == 0, total, total + new)
    total_out[...] = jnp.where(gets, new, summed)
    answer_out[...] = answer_ref[...] + new if step > 1 else new


def scan_kernel(n, step, *refs):
    place = lax.axis_index("seq")
    row = lax.axis_index("resp")
    prompt = row == 0
    count = n + 3 if step else n
    came = refs[:count]
    outs = refs[count : count + n]
    order, sums = refs[-2:]
    for m in range(n):
        order[jnp.bitwise_xor(place, m)] = came[m][...]
    if step:
        gets = jnp.logical_and(row >= step, row < 2 * step)
        total, new, answer = (ref[...] for ref in came[n:])
        forward = jnp.logical_not(prompt)
        before = jnp.where(prompt, answer + new, jnp.where(gets, new, total))
    else:
        forward = prompt
        before = jnp.zeros(order.shape[1:], F32)
    after = before
    for s in range(n):
        sums[s] = before
        before = before + order[s]
    for s in reversed(range(n)):
        sums[s] = jnp.where(forward, sums[s], after)
        after = after + order[s]
    for m in range(n):
        outs[m][...] = sums[jnp.bitwise_xor(place, m)]
    if not step:
        refs[count + n][...] = before


def per_device(n, rows, queries, keys, values, grad_out, lengths):
    tokens = queries.shape[1]
    width = queries.shape[2]
    factor = 1.0 / math.sqrt(2.0 * tokens * n)
    q, k, v, g = (x.reshape(tokens, width) for x in (queries, keys, values, grad_out))
    whole = pl.BlockSpec(memory_space=pltpu.VMEM)
    size = tokens * width

    def line(s, r):
        return s * rows + r

    def move(x, pairs):
        return lax.ppermute(x, AXES, pairs)

    there = pl.BlockSpec(memory_space=pltpu.HBM)
    array = pltpu.VMEM((tokens, width), BF16)
    stack = pltpu.VMEM((HEADS * HEAD, HEAD), F32)
    counts = pltpu.SMEM(lengths.shape, jnp.int32)
    piece = HEADS * HEAD // n
    piece_shape = jax.ShapeDtypeStruct((piece, HEAD), F32)
    small = pltpu.CompilerParams(vmem_limit_bytes=6 * 2**20)

    def far(x):
        return pltpu.with_memory_space_constraint(x, pltpu.HBM)

    *pieces, q, k, v, g = pl.pallas_call(
        functools.partial(state_kernel, n),
        in_specs=[there] * 5,
        out_specs=[whole] * (2 * n + 4),
        scratch_shapes=[stack] * 2 + [counts, pltpu.SemaphoreType.DMA((5,))],
        out_shape=[piece_shape] * (2 * n) + [jax.ShapeDtypeStruct((tokens, width), BF16)] * 4,
        compiler_params=pltpu.CompilerParams(vmem_limit_bytes=STATE_VMEM * 2**20),
        cost_estimate=pl.CostEstimate(
            flops=4 * size * HEAD, bytes_accessed=8 * size, transcendentals=0
        ),
    )(far(q), far(k), far(v), far(g), far(lengths))

    def swapped(pieces):
        came = [pieces[0]]
        for m in range(1, n):
            came.append(
                move(
                    pieces[m],
                    [(line(s, r), line(s ^ m, r)) for s in range(n) for r in range(rows)],
                )
            )
        return came

    def scan(step, *pieces):
        outputs = n if step else n + 1
        return pl.pallas_call(
            functools.partial(scan_kernel, n, step),
            in_specs=[whole] * len(pieces),
            out_specs=[whole] * outputs,
            out_shape=[piece_shape] * outputs,
            scratch_shapes=[pltpu.VMEM((n, piece, HEAD), F32)] * 2,
            compiler_params=small,
        )(*pieces)

    *share, total = scan(0, *swapped(pieces[:n]))
    rest = swapped(pieces[n:])
    share = swapped(share)
    answer = total
    step = 1
    while step < rows:
        pairs = [
            (line(s, at), line(s, at ^ step))
            for s in range(n)
            for at in range(rows)
            if at < step or (at % step == 0 and at & step)
        ]
        new = move(total, pairs)
        if 2 * step == rows:
            break
        total, answer = pl.pallas_call(
            functools.partial(step_kernel, step),
            in_specs=[whole] * 3,
            out_specs=[whole] * 2,
            out_shape=[piece_shape] * 2,
            compiler_params=small,
        )(total, new, answer)
        step *= 2
    rest = swapped(scan(step, *rest, total, new, answer))
    parts = []
    part_shape = jax.ShapeDtypeStruct((tokens, width // GROUPS), F32)
    for group in range(GROUPS):
        parts += pl.pallas_call(
            functools.partial(inner_kernel, factor, group * HEADS // GROUPS),
            in_specs=[whole] * 4,
            out_specs=[whole] * 4,
            out_shape=[part_shape] * 4,
            compiler_params=small,
            cost_estimate=pl.CostEstimate(
                flops=9 * size * tokens // GROUPS,
                bytes_accessed=24 * size // GROUPS,
                transcendentals=0,
            ),
        )(q, k, v, g)
    outs = pl.pallas_call(
        functools.partial(outer_kernel, factor, GROUPS, n),
        in_specs=[there] + [whole] * (4 + 4 * GROUPS + 2 * n),
        out_specs=[there] * 4,
        scratch_shapes=[array] * 4
        + [stack] * 2
        + [
            counts,
            pltpu.SemaphoreType.DMA((4, HEADS // WRITE)),
            pltpu.SemaphoreType.DMA,
        ],
        out_shape=[jax.ShapeDtypeStruct((tokens, width), BF16)] * 4,
        compiler_params=pltpu.CompilerParams(vmem_limit_bytes=12 * 2**20),
        cost_estimate=pl.CostEstimate(
            flops=8 * size * HEAD, bytes_accessed=32 * size, transcendentals=0
        ),
    )(far(lengths), q, k, v, g, *parts, *share, *rest)
    return tuple(x.reshape(1, tokens, width) for x in outs)


def solution(mesh):
    n = mesh.shape["seq"]
    spec = P("resp", "seq", None)

    def body(*args):
        return per_device(n, mesh.shape["resp"], *args)

    return jax.shard_map(
        body,
        mesh=mesh,
        in_specs=(spec, spec, spec, spec, P()),
        out_specs=(spec, spec, spec, spec),
        check_vma=False,
    )
```

```python
import functools
import math

import jax
import jax.numpy as jnp
from jax import lax
from jax.experimental import pallas as pl
from jax.experimental.pallas import tpu as pltpu
from jax.sharding import PartitionSpec as P


HEADS = 8
HEAD = 128
TILE = 256
GROUPS = 4
STATE_VMEM = 12
WRITE = 4
F32 = jnp.float32
BF16 = jnp.bfloat16
AXES = ("seq", "resp")

NN = (((1,), (0,)), ((), ()))
NT = (((1,), (1,)), ((), ()))
TN = (((0,), (0,)), ((), ()))


def dot(a, b, dims):
    return lax.dot_general(a, b, dims, preferred_element_type=F32)


def kept(lengths_ref):
    row = lax.axis_index("resp")
    limit = lengths_ref[jnp.maximum(row - 1, 0)]
    return jnp.logical_or(row == 0, lax.axis_index("seq") < limit)


def state_kernel(n, *refs):
    ins = refs[:5]
    share_refs = refs[5 : 5 + n]
    rest_refs = refs[5 + n : 5 + 2 * n]
    q_ref, k_ref, v_ref, g_ref = held = refs[5 + 2 * n : 9 + 2 * n]
    share, rest, lengths_ref, sem = refs[9 + 2 * n :]
    piece = share_refs[0].shape[0]
    counts = pltpu.make_async_copy(ins[4], lengths_ref, sem.at[4])
    counts.start()
    copies = [pltpu.make_async_copy(ins[i], held[i], sem.at[i]) for i in (1, 2, 0, 3)]
    for copy in copies:
        copy.start()
    place = lax.axis_index("seq")
    prompt = lax.axis_index("resp") == 0
    heads = [pl.ds(h * HEAD, HEAD) for h in range(HEADS)]
    counts.wait()
    keep = kept(lengths_ref)
    copies[0].wait()
    copies[1].wait()
    for h in heads:
        rest[h, :] = jnp.where(keep, dot(k_ref[:, h], v_ref[:, h], TN), 0.0)
    copies[2].wait()
    copies[3].wait()
    for h in heads:
        kv = rest[h, :]
        qg = jnp.where(keep, dot(q_ref[:, h], g_ref[:, h], TN), 0.0)
        share[h, :] = jnp.where(prompt, kv, qg)
        rest[h, :] = jnp.where(prompt, qg, kv)
    for m in range(n):
        at = pl.multiple_of(jnp.bitwise_xor(place, m) * piece, piece)
        share_refs[m][...] = share[pl.ds(at, piece), :]
        rest_refs[m][...] = rest[pl.ds(at, piece), :]


def inner_kernel(factor, first, q_ref, k_ref, v_ref, g_ref, *outs):
    tiles = q_ref.shape[0] // TILE
    cut = [pl.ds(i * TILE, TILE) for i in range(tiles)]
    rows = lax.broadcasted_iota(jnp.int32, (TILE, TILE), 0)
    columns = lax.broadcasted_iota(jnp.int32, (TILE, TILE), 1)
    causal = rows >= columns
    for h in range(outs[0].shape[1] // HEAD):
        here = pl.ds((first + h) * HEAD, HEAD)
        q, k, v, g = ([ref[c, here] for c in cut] for ref in (q_ref, k_ref, v_ref, g_ref))
        sums = [[None] * tiles for _ in range(4)]

        def add(which, at, term):
            old = sums[which][at]
            sums[which][at] = term if old is None else old + term

        for i in range(tiles):
            for j in range(i + 1):
                a = dot(q[i], k[j], NT) * factor
                p = dot(g[i], v[j], NT) * factor
                if i == j:
                    a = jnp.where(causal, a, 0.0)
                    p = jnp.where(causal, p, 0.0)
                a = a.astype(BF16)
                p = p.astype(BF16)
                add(0, i, dot(a, v[j], NN))
                add(1, i, dot(p, k[j], NN))
                add(2, j, dot(p, q[i], TN))
                add(3, j, dot(a, g[i], TN))
        for ref, parts in zip(outs, sums):
            for c, part in zip(cut, parts):
                ref[c, pl.ds(h * HEAD, HEAD)] = part


def outer_kernel(factor, groups, n, first, lengths_hbm, *refs):
    arrays = refs[:4]
    parts = refs[4 : 4 + 4 * groups]
    refs = refs[4 + 4 * groups :]
    pieces = refs[:n]
    outs = refs[n : n + 4] if first else refs[n + 4 : n + 8]
    buffers = refs[-6:-4]
    state, lengths_ref, sem, count_sem = refs[-4:]
    counts = pltpu.make_async_copy(lengths_hbm, lengths_ref, count_sem)
    counts.start()
    place = lax.axis_index("seq")
    prompt = lax.axis_index("resp") == 0
    piece = pieces[0].shape[0]
    for m in range(n):
        at = pl.multiple_of(jnp.bitwise_xor(place, m) * piece, piece)
        state[pl.ds(at, piece), :] = pieces[m][...]
    counts.wait()
    keep = kept(lengths_ref)
    span = HEADS // groups

    def write(sides):
        copies = []
        for head in range(HEADS):
            h = pl.ds(head * HEAD, HEAD)
            within = pl.ds(head % span * HEAD, HEAD)
            low = state[h, :].astype(BF16)
            for buffer, (which, source, dims) in zip(buffers, sides):
                part = parts[head // span * 4 + which][:, within]
                total = part + factor * dot(arrays[source][:, h], low, dims)
                buffer[:, h] = jnp.where(keep, total, 0.0).astype(BF16)
            if head % WRITE == WRITE - 1:
                at = head // WRITE
                wide = pl.ds(at * WRITE * HEAD, WRITE * HEAD)
                for i, (which, _, _) in enumerate(sides):
                    copy = pltpu.make_async_copy(
                        buffers[i].at[:, wide], outs[which].at[:, wide], sem.at[i, at]
                    )
                    copy.start()
                    copies.append(copy)
        for copy in copies:
            copy.wait()

    @pl.when(prompt == first)
    def _():
        write(((0, 0, NN), (1, 3, NT)))

    @pl.when(prompt != first)
    def _():
        write(((2, 2, NT), (3, 1, NN)))


def pair_kernel(mine_ref, new_ref, send_ref, sum_ref):
    row = lax.axis_index("resp")
    mine = mine_ref[...]
    new = new_ref[...]
    both = mine + new
    send_ref[...] = jnp.where(row == 0, mine, jnp.where(row == 1, new, both))
    sum_ref[...] = jnp.where(row == 0, new, mine)


def level_kernel(layers, send_ref, sum_ref, *refs):
    row = lax.axis_index("resp")
    layer = lax.div(row, 2)
    answer = sum_ref[...]
    prompt = jnp.zeros_like(answer)
    for k in range(1, layers):
        new = refs[k - 1][...]
        answer = answer + new
        prompt = prompt + jnp.where(layer == k, new, 0.0)
    total = jnp.where(layer == 0, answer, prompt)
    send = send_ref[...]
    own_ref, give_ref = refs[-2:]
    own_ref[...] = jnp.where(row == 1, send, total)
    give_ref[...] = jnp.where(row == 0, send, total)


def scan_kernel(n, first, *refs):
    place = lax.axis_index("seq")
    row = lax.axis_index("resp")
    prompt = row == 0
    count = n if first else n + 2
    came = refs[:count]
    outs = refs[count : count + n]
    order, sums = refs[-2:]
    for m in range(n):
        order[jnp.bitwise_xor(place, m)] = came[m][...]
    core = lax.rem(row, 2)
    half = came[-1].shape[0] if not first else refs[count + n].shape[0]
    here = pl.ds(pl.multiple_of(core * half, half), half)
    there = pl.ds(pl.multiple_of((1 - core) * half, half), half)
    if first:
        forward = prompt
        before = jnp.zeros(order.shape[1:], F32)
    else:
        forward = jnp.logical_not(prompt)
        sums[0, here, :] = came[n][...]
        sums[0, there, :] = came[n + 1][...]
        before = sums[0]
    after = before
    for s in range(n):
        sums[s] = before
        before = before + order[s]
    for s in reversed(range(n)):
        sums[s] = jnp.where(forward, sums[s], after)
        after = after + order[s]
    for m in range(n):
        outs[m][...] = sums[jnp.bitwise_xor(place, m)]
    if first:
        order[0] = before
        refs[count + n][...] = order[0, here, :]
        refs[count + n + 1][...] = order[0, there, :]


def per_device(n, rows, queries, keys, values, grad_out, lengths):
    tokens = queries.shape[1]
    width = queries.shape[2]
    factor = 1.0 / math.sqrt(2.0 * tokens * n)
    q, k, v, g = (x.reshape(tokens, width) for x in (queries, keys, values, grad_out))
    whole = pl.BlockSpec(memory_space=pltpu.VMEM)
    size = tokens * width

    def line(s, r):
        return s * rows + r

    def move(x, pairs):
        return lax.ppermute(x, AXES, pairs)

    there = pl.BlockSpec(memory_space=pltpu.HBM)
    array = pltpu.VMEM((tokens, width), BF16)
    stack = pltpu.VMEM((HEADS * HEAD, HEAD), F32)
    counts = pltpu.SMEM(lengths.shape, jnp.int32)
    piece = HEADS * HEAD // n
    piece_shape = jax.ShapeDtypeStruct((piece, HEAD), F32)
    half_shape = jax.ShapeDtypeStruct((piece // 2, HEAD), F32)
    small = pltpu.CompilerParams(vmem_limit_bytes=6 * 2**20)

    def far(x):
        return pltpu.with_memory_space_constraint(x, pltpu.HBM)

    *pieces, q, k, v, g = pl.pallas_call(
        functools.partial(state_kernel, n),
        in_specs=[there] * 5,
        out_specs=[whole] * (2 * n + 4),
        scratch_shapes=[stack] * 2 + [counts, pltpu.SemaphoreType.DMA((5,))],
        out_shape=[piece_shape] * (2 * n) + [jax.ShapeDtypeStruct((tokens, width), BF16)] * 4,
        compiler_params=pltpu.CompilerParams(vmem_limit_bytes=STATE_VMEM * 2**20),
        cost_estimate=pl.CostEstimate(
            flops=4 * size * HEAD, bytes_accessed=8 * size, transcendentals=0
        ),
    )(far(q), far(k), far(v), far(g), far(lengths))

    def swapped(pieces):
        came = [pieces[0]]
        for m in range(1, n):
            came.append(
                move(
                    pieces[m],
                    [(line(s, r), line(s ^ m, r)) for s in range(n) for r in range(rows)],
                )
            )
        return came

    def scan(first, *pieces):
        shapes = [piece_shape] * n + [half_shape] * (2 * first)
        return pl.pallas_call(
            functools.partial(scan_kernel, n, first),
            in_specs=[whole] * len(pieces),
            out_specs=[whole] * len(shapes),
            out_shape=shapes,
            scratch_shapes=[pltpu.VMEM((n, piece, HEAD), F32)] * 2,
            compiler_params=small,
        )(*pieces)

    *share, mine, give = scan(True, *swapped(pieces[:n]))
    rest = swapped(pieces[n:])
    share = swapped(share)

    def across(x, bits):
        return move(x, [(line(s, r), line(s, r ^ bits)) for s in range(n) for r in range(rows)])

    def combine(kernel, *inputs):
        return pl.pallas_call(
            kernel,
            in_specs=[whole] * len(inputs),
            out_specs=[whole] * 2,
            out_shape=[half_shape] * 2,
            compiler_params=small,
        )(*inputs)

    layers = rows // 2
    send, gathered = combine(pair_kernel, mine, across(give, 1))
    levels = [across(send, 2 * k) for k in range(1, layers)]
    own, give = combine(functools.partial(level_kernel, layers), send, gathered, *levels)
    new = across(give, 1)
    rest = swapped(scan(False, *rest, own, new))
    parts = []
    part_shape = jax.ShapeDtypeStruct((tokens, width // GROUPS), F32)
    for group in range(GROUPS):
        parts += pl.pallas_call(
            functools.partial(inner_kernel, factor, group * HEADS // GROUPS),
            in_specs=[whole] * 4,
            out_specs=[whole] * 4,
            out_shape=[part_shape] * 4,
            compiler_params=small,
            cost_estimate=pl.CostEstimate(
                flops=9 * size * tokens // GROUPS,
                bytes_accessed=24 * size // GROUPS,
                transcendentals=0,
            ),
        )(q, k, v, g)
    outs = []
    for first, pieces in ((True, share), (False, rest)):
        fixed = 5 + 4 * GROUPS + n
        outs = pl.pallas_call(
            functools.partial(outer_kernel, factor, GROUPS, n, first),
            in_specs=[there] + [whole] * (fixed - 1) + [there] * len(outs),
            out_specs=[there] * 4,
            scratch_shapes=[array] * 2
            + [
                stack,
                counts,
                pltpu.SemaphoreType.DMA((2, HEADS // WRITE)),
                pltpu.SemaphoreType.DMA,
            ],
            out_shape=[jax.ShapeDtypeStruct((tokens, width), BF16)] * 4,
            input_output_aliases={fixed + i: i for i in range(len(outs))},
            compiler_params=pltpu.CompilerParams(vmem_limit_bytes=8 * 2**20),
            cost_estimate=pl.CostEstimate(
                flops=4 * size * HEAD, bytes_accessed=16 * size, transcendentals=0
            ),
        )(far(lengths), q, k, v, g, *parts, *pieces, *outs)
    return tuple(x.reshape(1, tokens, width) for x in outs)


def solution(mesh):
    n = mesh.shape["seq"]
    spec = P("resp", "seq", None)

    def body(*args):
        return per_device(n, mesh.shape["resp"], *args)

    return jax.shard_map(
        body,
        mesh=mesh,
        in_specs=(spec, spec, spec, spec, P()),
        out_specs=(spec, spec, spec, spec),
        check_vma=False,
    )
```

```python
import functools
import math

import jax
import jax.numpy as jnp
from jax import lax
from jax.experimental import pallas as pl
from jax.experimental.pallas import tpu as pltpu
from jax.sharding import PartitionSpec as P


HEADS = 8
HEAD = 128
TILE = 256
GROUPS = 4
STATE_VMEM = 12
WRITE = 2
F32 = jnp.float32
BF16 = jnp.bfloat16
AXES = ("seq", "resp")

NN = (((1,), (0,)), ((), ()))
NT = (((1,), (1,)), ((), ()))
TN = (((0,), (0,)), ((), ()))


def dot(a, b, dims):
    return lax.dot_general(a, b, dims, preferred_element_type=F32)


def kept(lengths_ref):
    row = lax.axis_index("resp")
    limit = lengths_ref[jnp.maximum(row - 1, 0)]
    return jnp.logical_or(row == 0, lax.axis_index("seq") < limit)


def state_kernel(n, *refs):
    ins = refs[:5]
    share_refs = refs[5 : 5 + n]
    rest_refs = refs[5 + n : 5 + 2 * n]
    q_ref, k_ref, v_ref, g_ref = held = refs[5 + 2 * n : 9 + 2 * n]
    share, rest, lengths_ref, sem = refs[9 + 2 * n :]
    piece = share_refs[0].shape[0]
    counts = pltpu.make_async_copy(ins[4], lengths_ref, sem.at[4])
    counts.start()
    copies = [pltpu.make_async_copy(ins[i], held[i], sem.at[i]) for i in (1, 2, 0, 3)]
    for copy in copies:
        copy.start()
    place = lax.axis_index("seq")
    prompt = lax.axis_index("resp") == 0
    heads = [pl.ds(h * HEAD, HEAD) for h in range(HEADS)]
    counts.wait()
    keep = kept(lengths_ref)
    copies[0].wait()
    copies[1].wait()
    for h in heads:
        rest[h, :] = jnp.where(keep, dot(k_ref[:, h], v_ref[:, h], TN), 0.0)
    copies[2].wait()
    copies[3].wait()
    for h in heads:
        kv = rest[h, :]
        qg = jnp.where(keep, dot(q_ref[:, h], g_ref[:, h], TN), 0.0)
        share[h, :] = jnp.where(prompt, kv, qg)
        rest[h, :] = jnp.where(prompt, qg, kv)
    for m in range(n):
        at = pl.multiple_of(jnp.bitwise_xor(place, m) * piece, piece)
        share_refs[m][...] = share[pl.ds(at, piece), :]
        rest_refs[m][...] = rest[pl.ds(at, piece), :]


def inner_kernel(factor, first, q_ref, k_ref, v_ref, g_ref, *outs):
    tiles = q_ref.shape[0] // TILE
    cut = [pl.ds(i * TILE, TILE) for i in range(tiles)]
    rows = lax.broadcasted_iota(jnp.int32, (TILE, TILE), 0)
    columns = lax.broadcasted_iota(jnp.int32, (TILE, TILE), 1)
    causal = rows >= columns
    for h in range(outs[0].shape[1] // HEAD):
        here = pl.ds((first + h) * HEAD, HEAD)
        q, k, v, g = ([ref[c, here] for c in cut] for ref in (q_ref, k_ref, v_ref, g_ref))
        sums = [[None] * tiles for _ in range(4)]

        def add(which, at, term):
            old = sums[which][at]
            sums[which][at] = term if old is None else old + term

        for i in range(tiles):
            for j in range(i + 1):
                a = dot(q[i], k[j], NT) * factor
                p = dot(g[i], v[j], NT) * factor
                if i == j:
                    a = jnp.where(causal, a, 0.0)
                    p = jnp.where(causal, p, 0.0)
                a = a.astype(BF16)
                p = p.astype(BF16)
                add(0, i, dot(a, v[j], NN))
                add(1, i, dot(p, k[j], NN))
                add(2, j, dot(p, q[i], TN))
                add(3, j, dot(a, g[i], TN))
        for ref, parts in zip(outs, sums):
            for c, part in zip(cut, parts):
                ref[c, pl.ds(h * HEAD, HEAD)] = part


def outer_kernel(factor, groups, n, first, lengths_hbm, *refs):
    arrays = refs[:4]
    parts = refs[4 : 4 + 4 * groups]
    refs = refs[4 + 4 * groups :]
    pieces = refs[:n]
    outs = refs[n : n + 4] if first else refs[n + 4 : n + 8]
    buffers = refs[-6:-4]
    state, lengths_ref, sem, count_sem = refs[-4:]
    counts = pltpu.make_async_copy(lengths_hbm, lengths_ref, count_sem)
    counts.start()
    place = lax.axis_index("seq")
    prompt = lax.axis_index("resp") == 0
    piece = pieces[0].shape[0]
    for m in range(n):
        at = pl.multiple_of(jnp.bitwise_xor(place, m) * piece, piece)
        state[pl.ds(at, piece), :] = pieces[m][...]
    counts.wait()
    keep = kept(lengths_ref)
    span = HEADS // groups

    def write(sides):
        copies = []
        for head in range(HEADS):
            h = pl.ds(head * HEAD, HEAD)
            within = pl.ds(head % span * HEAD, HEAD)
            low = state[h, :].astype(BF16)
            for buffer, (which, source, dims) in zip(buffers, sides):
                part = parts[head // span * 4 + which][:, within]
                total = part + factor * dot(arrays[source][:, h], low, dims)
                buffer[:, h] = jnp.where(keep, total, 0.0).astype(BF16)
            if head % WRITE == WRITE - 1:
                at = head // WRITE
                wide = pl.ds(at * WRITE * HEAD, WRITE * HEAD)
                for i, (which, _, _) in enumerate(sides):
                    copy = pltpu.make_async_copy(
                        buffers[i].at[:, wide], outs[which].at[:, wide], sem.at[i, at]
                    )
                    copy.start()
                    copies.append(copy)
        for copy in copies:
            copy.wait()

    @pl.when(prompt == first)
    def _():
        write(((0, 0, NN), (1, 3, NT)))

    @pl.when(prompt != first)
    def _():
        write(((2, 2, NT), (3, 1, NN)))


def pair_kernel(mine_ref, new_ref, send_ref, sum_ref):
    row = lax.axis_index("resp")
    mine = mine_ref[...]
    new = new_ref[...]
    both = mine + new
    send_ref[...] = jnp.where(row == 0, mine, jnp.where(row == 1, new, both))
    sum_ref[...] = jnp.where(row == 0, new, mine)


def level_kernel(layers, send_ref, sum_ref, *refs):
    row = lax.axis_index("resp")
    layer = lax.div(row, 2)
    answer = sum_ref[...]
    prompt = jnp.zeros_like(answer)
    for k in range(1, layers):
        new = refs[k - 1][...]
        answer = answer + new
        prompt = prompt + jnp.where(layer == k, new, 0.0)
    total = jnp.where(layer == 0, answer, prompt)
    send = send_ref[...]
    own_ref, give_ref = refs[-2:]
    own_ref[...] = jnp.where(row == 1, send, total)
    give_ref[...] = jnp.where(row == 0, send, total)


def scan_kernel(n, first, *refs):
    place = lax.axis_index("seq")
    row = lax.axis_index("resp")
    prompt = row == 0
    count = n if first else n + 2
    came = refs[:count]
    outs = refs[count : count + n]
    order, sums = refs[-2:]
    for m in range(n):
        order[jnp.bitwise_xor(place, m)] = came[m][...]
    core = lax.rem(row, 2)
    half = came[-1].shape[0] if not first else refs[count + n].shape[0]
    here = pl.ds(pl.multiple_of(core * half, half), half)
    there = pl.ds(pl.multiple_of((1 - core) * half, half), half)
    if first:
        forward = prompt
        before = jnp.zeros(order.shape[1:], F32)
    else:
        forward = jnp.logical_not(prompt)
        sums[0, here, :] = came[n][...]
        sums[0, there, :] = came[n + 1][...]
        before = sums[0]
    after = before
    for s in range(n):
        sums[s] = before
        before = before + order[s]
    for s in reversed(range(n)):
        sums[s] = jnp.where(forward, sums[s], after)
        after = after + order[s]
    for m in range(n):
        outs[m][...] = sums[jnp.bitwise_xor(place, m)]
    if first:
        order[0] = before
        refs[count + n][...] = order[0, here, :]
        refs[count + n + 1][...] = order[0, there, :]


def per_device(n, rows, queries, keys, values, grad_out, lengths):
    tokens = queries.shape[1]
    width = queries.shape[2]
    factor = 1.0 / math.sqrt(2.0 * tokens * n)
    q, k, v, g = (x.reshape(tokens, width) for x in (queries, keys, values, grad_out))
    whole = pl.BlockSpec(memory_space=pltpu.VMEM)
    size = tokens * width

    def line(s, r):
        return s * rows + r

    def move(x, pairs):
        return lax.ppermute(x, AXES, pairs)

    there = pl.BlockSpec(memory_space=pltpu.HBM)
    array = pltpu.VMEM((tokens, width), BF16)
    stack = pltpu.VMEM((HEADS * HEAD, HEAD), F32)
    counts = pltpu.SMEM(lengths.shape, jnp.int32)
    piece = HEADS * HEAD // n
    piece_shape = jax.ShapeDtypeStruct((piece, HEAD), F32)
    half_shape = jax.ShapeDtypeStruct((piece // 2, HEAD), F32)
    small = pltpu.CompilerParams(vmem_limit_bytes=6 * 2**20)

    def far(x):
        return pltpu.with_memory_space_constraint(x, pltpu.HBM)

    *pieces, q, k, v, g = pl.pallas_call(
        functools.partial(state_kernel, n),
        in_specs=[there] * 5,
        out_specs=[whole] * (2 * n + 4),
        scratch_shapes=[stack] * 2 + [counts, pltpu.SemaphoreType.DMA((5,))],
        out_shape=[piece_shape] * (2 * n) + [jax.ShapeDtypeStruct((tokens, width), BF16)] * 4,
        compiler_params=pltpu.CompilerParams(vmem_limit_bytes=STATE_VMEM * 2**20),
        cost_estimate=pl.CostEstimate(
            flops=4 * size * HEAD, bytes_accessed=8 * size, transcendentals=0
        ),
    )(far(q), far(k), far(v), far(g), far(lengths))

    def swapped(pieces):
        came = [pieces[0]]
        for m in range(1, n):
            came.append(
                move(
                    pieces[m],
                    [(line(s, r), line(s ^ m, r)) for s in range(n) for r in range(rows)],
                )
            )
        return came

    def scan(first, *pieces):
        shapes = [piece_shape] * n + [half_shape] * (2 * first)
        return pl.pallas_call(
            functools.partial(scan_kernel, n, first),
            in_specs=[whole] * len(pieces),
            out_specs=[whole] * len(shapes),
            out_shape=shapes,
            scratch_shapes=[pltpu.VMEM((n, piece, HEAD), F32)] * 2,
            compiler_params=small,
        )(*pieces)

    *share, mine, give = scan(True, *swapped(pieces[:n]))
    rest = swapped(pieces[n:])
    share = swapped(share)

    def across(x, bits):
        return move(x, [(line(s, r), line(s, r ^ bits)) for s in range(n) for r in range(rows)])

    def combine(kernel, *inputs):
        return pl.pallas_call(
            kernel,
            in_specs=[whole] * len(inputs),
            out_specs=[whole] * 2,
            out_shape=[half_shape] * 2,
            compiler_params=small,
        )(*inputs)

    layers = rows // 2
    send, gathered = combine(pair_kernel, mine, across(give, 1))
    levels = []
    for z in range(1, layers):
        meets = {0: z, z: 0}
        pairs = [
            (line(s, r), line(s, 2 * meets[r // 2] + r % 2 if r // 2 in meets else r ^ 1))
            for s in range(n)
            for r in range(rows)
        ]
        levels.append(move(send, pairs))
    own, give = combine(functools.partial(level_kernel, layers), send, gathered, *levels)
    new = across(give, 1)
    rest = swapped(scan(False, *rest, own, new))
    parts = []
    part_shape = jax.ShapeDtypeStruct((tokens, width // GROUPS), F32)
    for group in range(GROUPS):
        parts += pl.pallas_call(
            functools.partial(inner_kernel, factor, group * HEADS // GROUPS),
            in_specs=[whole] * 4,
            out_specs=[whole] * 4,
            out_shape=[part_shape] * 4,
            compiler_params=small,
            cost_estimate=pl.CostEstimate(
                flops=9 * size * tokens // GROUPS,
                bytes_accessed=24 * size // GROUPS,
                transcendentals=0,
            ),
        )(q, k, v, g)
    outs = []
    for first, pieces in ((True, share), (False, rest)):
        fixed = 5 + 4 * GROUPS + n
        outs = pl.pallas_call(
            functools.partial(outer_kernel, factor, GROUPS, n, first),
            in_specs=[there] + [whole] * (fixed - 1) + [there] * len(outs),
            out_specs=[there] * 4,
            scratch_shapes=[array] * 2
            + [
                stack,
                counts,
                pltpu.SemaphoreType.DMA((2, HEADS // WRITE)),
                pltpu.SemaphoreType.DMA,
            ],
            out_shape=[jax.ShapeDtypeStruct((tokens, width), BF16)] * 4,
            input_output_aliases={fixed + i: i for i in range(len(outs))},
            compiler_params=pltpu.CompilerParams(vmem_limit_bytes=8 * 2**20),
            cost_estimate=pl.CostEstimate(
                flops=4 * size * HEAD, bytes_accessed=16 * size, transcendentals=0
            ),
        )(far(lengths), q, k, v, g, *parts, *pieces, *outs)
    return tuple(x.reshape(1, tokens, width) for x in outs)


def solution(mesh):
    n = mesh.shape["seq"]
    spec = P("resp", "seq", None)

    def body(*args):
        return per_device(n, mesh.shape["resp"], *args)

    return jax.shard_map(
        body,
        mesh=mesh,
        in_specs=(spec, spec, spec, spec, P()),
        out_specs=(spec, spec, spec, spec),
        check_vma=False,
    )
```

```python
import functools
import math

import jax
import jax.numpy as jnp
from jax import lax
from jax.experimental import pallas as pl
from jax.experimental.pallas import tpu as pltpu
from jax.sharding import PartitionSpec as P


HEADS = 8
HEAD = 128
TILE = 256
GROUPS = 4
STATE_VMEM = 8
WRITE = 4
F32 = jnp.float32
BF16 = jnp.bfloat16
AXES = ("seq", "resp")

NN = (((1,), (0,)), ((), ()))
NT = (((1,), (1,)), ((), ()))
TN = (((0,), (0,)), ((), ()))


def dot(a, b, dims):
    return lax.dot_general(a, b, dims, preferred_element_type=F32)


def kept(lengths_ref):
    row = lax.axis_index("resp")
    limit = lengths_ref[jnp.maximum(row - 1, 0)]
    return jnp.logical_or(row == 0, lax.axis_index("seq") < limit)


def state_kernel(n, tiles, share, lengths_hbm, *refs):
    prompt = lax.axis_index("resp") == 0
    keys_values = prompt == share
    sources = refs[:4]
    piece_refs = refs[4 : 4 + n]
    held = refs[4 + n : 6 + n]
    sums = refs[6 + n : 5 + n + tiles]
    total, lengths_ref, sem, count_sem = refs[-4:]
    piece = piece_refs[0].shape[0]
    counts = pltpu.make_async_copy(lengths_hbm, lengths_ref, count_sem)
    cut = [pl.ds(i * TILE, TILE) for i in range(tiles)]

    def copies(pair):
        return [
            [pltpu.make_async_copy(pair[x].at[c], held[x].at[c], sem.at[x, i]) for x in (0, 1)]
            for i, c in enumerate(cut)
        ]

    def start(pair):
        for tile in copies(pair):
            for copy in tile:
                copy.start()

    counts.start()

    @pl.when(keys_values)
    def _():
        start(sources[:2])

    @pl.when(jnp.logical_not(keys_values))
    def _():
        start(sources[2:])

    waits = copies(sources[:2])
    place = lax.axis_index("seq")
    heads = [pl.ds(h * HEAD, HEAD) for h in range(HEADS)]
    for i in range(tiles):
        if i == 0:
            counts.wait()
        for copy in waits[i]:
            copy.wait()

        @pl.when(jnp.logical_not(kept(lengths_ref)))
        def _():
            for ref in held:
                ref[cut[i], :] = jnp.zeros((TILE, ref.shape[1]), BF16)

        for h in heads:
            new = dot(held[0][cut[i], h], held[1][cut[i], h], TN)
            if i < tiles - 1:
                sums[i][h, :] = new
                continue
            parts = [ref[h, :] for ref in sums] + [new]
            whole = sum(parts[1:], parts[0])
            upto = None
            for ref, part in zip(sums, parts):
                upto = part if upto is None else upto + part
                ref[h, :] = jnp.where(keys_values, upto, whole - upto if tiles > 2 else new)
            total[h, :] = whole
    for m in range(n):
        at = pl.multiple_of(jnp.bitwise_xor(place, m) * piece, piece)
        piece_refs[m][...] = total[pl.ds(at, piece), :]


def inner_kernel(factor, first, *refs):
    outs = refs[4:]
    rows = lax.broadcasted_iota(jnp.int32, (TILE, TILE), 0)
    columns = lax.broadcasted_iota(jnp.int32, (TILE, TILE), 1)
    causal = rows >= columns

    def write(arrays):
        for h in range(outs[0].shape[1] // HEAD):
            here = pl.ds((first + h) * HEAD, HEAD)
            there = pl.ds(h * HEAD, HEAD)
            for i in range(arrays[0].shape[0] // TILE):
                c = pl.ds(i * TILE, TILE)
                q, k, v, g = (ref[c, here] for ref in arrays)
                a = jnp.where(causal, dot(q, k, NT) * factor, 0.0).astype(BF16)
                p = jnp.where(causal, dot(g, v, NT) * factor, 0.0).astype(BF16)
                outs[0][c, there] = dot(a, v, NN)
                outs[1][c, there] = dot(p, k, NN)
                outs[2][c, there] = dot(p, q, TN)
                outs[3][c, there] = dot(a, g, TN)

    prompt = lax.axis_index("resp") == 0
    a, b, c, d = refs[:4]

    @pl.when(prompt)
    def _():
        write((c, a, b, d))

    @pl.when(jnp.logical_not(prompt))
    def _():
        write((a, c, d, b))


def outer_kernel(factor, groups, n, tiles, first, *refs):
    arrays = refs[:2]
    parts = refs[2 : 2 + 4 * groups]
    refs = refs[2 + 4 * groups :]
    pieces = refs[:n]
    sums = refs[n : n + tiles - 1]
    refs = refs[n + tiles - 1 :]
    outs = refs[:4] if first else refs[4:8]
    buffers = refs[-4:-2]
    state, sem = refs[-2:]
    place = lax.axis_index("seq")
    prompt = lax.axis_index("resp") == 0
    piece = pieces[0].shape[0]
    for m in range(n):
        at = pl.multiple_of(jnp.bitwise_xor(place, m) * piece, piece)
        state[pl.ds(at, piece), :] = pieces[m][...]
    span = HEADS // groups

    def write(sides, added):
        copies = []
        for tile in range(tiles):
            c = pl.ds(tile * TILE, TILE)
            for head in range(HEADS):
                h = pl.ds(head * HEAD, HEAD)
                within = pl.ds(head % span * HEAD, HEAD)
                total = state[h, :]
                if added[tile] is not None:
                    total = total + added[tile][h, :]
                low = total.astype(BF16)
                for buffer, (which, source, dims) in zip(buffers, sides):
                    part = parts[head // span * 4 + which][c, within]
                    out = part + factor * dot(arrays[source][c, h], low, dims)
                    buffer[c, h] = out.astype(BF16)
                if head % WRITE == WRITE - 1:
                    at = head // WRITE
                    wide = pl.ds(at * WRITE * HEAD, WRITE * HEAD)
                    for i, (which, _, _) in enumerate(sides):
                        copy = pltpu.make_async_copy(
                            buffers[i].at[c, wide], outs[which].at[c, wide], sem.at[i, tile, at]
                        )
                        copy.start()
                        copies.append(copy)
        for copy in copies:
            copy.wait()

    @pl.when(prompt == first)
    def _():
        write(((0, 0, NN), (1, 1, NT)), (None, *sums))

    @pl.when(prompt != first)
    def _():
        write(((2, 1, NT), (3, 0, NN)), (*sums, None))


def pair_kernel(mine_ref, new_ref, send_ref, sum_ref):
    row = lax.axis_index("resp")
    mine = mine_ref[...]
    new = new_ref[...]
    both = mine + new
    send_ref[...] = jnp.where(row == 0, mine, jnp.where(row == 1, new, both))
    sum_ref[...] = jnp.where(row == 0, new, mine)


def level_kernel(layers, send_ref, sum_ref, *refs):
    row = lax.axis_index("resp")
    layer = lax.div(row, 2)
    answer = sum_ref[...]
    prompt = jnp.zeros_like(answer)
    for k in range(1, layers):
        new = refs[k - 1][...]
        answer = answer + new
        prompt = prompt + jnp.where(layer == k, new, 0.0)
    total = jnp.where(layer == 0, answer, prompt)
    send = send_ref[...]
    own_ref, give_ref = refs[-2:]
    own_ref[...] = jnp.where(row == 1, send, total)
    give_ref[...] = jnp.where(row == 0, send, total)


def scan_kernel(n, first, *refs):
    place = lax.axis_index("seq")
    row = lax.axis_index("resp")
    prompt = row == 0
    count = n if first else n + 2
    came = refs[:count]
    outs = refs[count : count + n]
    order, sums = refs[-2:]
    for m in range(n):
        order[jnp.bitwise_xor(place, m)] = came[m][...]
    core = lax.rem(row, 2)
    half = came[-1].shape[0] if not first else refs[count + n].shape[0]
    here = pl.ds(pl.multiple_of(core * half, half), half)
    there = pl.ds(pl.multiple_of((1 - core) * half, half), half)
    if first:
        forward = prompt
        before = jnp.zeros(order.shape[1:], F32)
    else:
        forward = jnp.logical_not(prompt)
        sums[0, here, :] = came[n][...]
        sums[0, there, :] = came[n + 1][...]
        before = sums[0]
    after = before
    for s in range(n):
        sums[s] = before
        before = before + order[s]
    for s in reversed(range(n)):
        sums[s] = jnp.where(forward, sums[s], after)
        after = after + order[s]
    for m in range(n):
        outs[m][...] = sums[jnp.bitwise_xor(place, m)]
    if first:
        order[0] = before
        refs[count + n][...] = order[0, here, :]
        refs[count + n + 1][...] = order[0, there, :]


def per_device(n, rows, queries, keys, values, grad_out, lengths):
    tokens = queries.shape[1]
    width = queries.shape[2]
    factor = 1.0 / math.sqrt(2.0 * tokens * n)
    q, k, v, g = (x.reshape(tokens, width) for x in (queries, keys, values, grad_out))
    whole = pl.BlockSpec(memory_space=pltpu.VMEM)
    size = tokens * width

    def line(s, r):
        return s * rows + r

    def move(x, pairs):
        return lax.ppermute(x, AXES, pairs)

    there = pl.BlockSpec(memory_space=pltpu.HBM)
    array = pltpu.VMEM((tokens, width), BF16)
    stack = pltpu.VMEM((HEADS * HEAD, HEAD), F32)
    counts = pltpu.SMEM(lengths.shape, jnp.int32)
    tiles = tokens // TILE
    piece = HEADS * HEAD // n
    piece_shape = jax.ShapeDtypeStruct((piece, HEAD), F32)
    half_shape = jax.ShapeDtypeStruct((piece // 2, HEAD), F32)
    small = pltpu.CompilerParams(vmem_limit_bytes=6 * 2**20)

    def far(x):
        return pltpu.with_memory_space_constraint(x, pltpu.HBM)

    def state(share):
        made = pl.pallas_call(
            functools.partial(state_kernel, n, tiles, share),
            in_specs=[there] * 5,
            out_specs=[whole] * (n + 1 + tiles),
            scratch_shapes=[
                stack,
                counts,
                pltpu.SemaphoreType.DMA((2, tiles)),
                pltpu.SemaphoreType.DMA,
            ],
            out_shape=[piece_shape] * n
            + [jax.ShapeDtypeStruct((tokens, width), BF16)] * 2
            + [jax.ShapeDtypeStruct((HEADS * HEAD, HEAD), F32)] * (tiles - 1),
            compiler_params=pltpu.CompilerParams(vmem_limit_bytes=STATE_VMEM * 2**20),
            cost_estimate=pl.CostEstimate(
                flops=2 * size * HEAD, bytes_accessed=4 * size, transcendentals=0
            ),
        )(far(lengths), far(k), far(v), far(q), far(g))
        return made[:n], made[n : n + 2], made[n + 2 :]

    share, share_arrays, share_sums = state(True)
    rest, rest_arrays, rest_sums = state(False)

    def swapped(pieces):
        came = [pieces[0]]
        for m in range(1, n):
            came.append(
                move(
                    pieces[m],
                    [(line(s, r), line(s ^ m, r)) for s in range(n) for r in range(rows)],
                )
            )
        return came

    def scan(first, *pieces):
        shapes = [piece_shape] * n + [half_shape] * (2 * first)
        return pl.pallas_call(
            functools.partial(scan_kernel, n, first),
            in_specs=[whole] * len(pieces),
            out_specs=[whole] * len(shapes),
            out_shape=shapes,
            scratch_shapes=[pltpu.VMEM((n, piece, HEAD), F32)] * 2,
            compiler_params=small,
        )(*pieces)

    *share, mine, give = scan(True, *swapped(share))
    rest = swapped(rest)
    share = swapped(share)

    def across(x, bits):
        return move(x, [(line(s, r), line(s, r ^ bits)) for s in range(n) for r in range(rows)])

    def combine(kernel, *inputs):
        return pl.pallas_call(
            kernel,
            in_specs=[whole] * len(inputs),
            out_specs=[whole] * 2,
            out_shape=[half_shape] * 2,
            compiler_params=small,
        )(*inputs)

    layers = rows // 2
    send, gathered = combine(pair_kernel, mine, across(give, 1))
    levels = []
    for z in range(1, layers):
        meets = {0: z, z: 0}
        pairs = [
            (line(s, r), line(s, 2 * meets[r // 2] + r % 2 if r // 2 in meets else r ^ 1))
            for s in range(n)
            for r in range(rows)
        ]
        levels.append(move(send, pairs))
    own, give = combine(functools.partial(level_kernel, layers), send, gathered, *levels)
    new = across(give, 1)
    rest = swapped(scan(False, *rest, own, new))
    parts = []
    part_shape = jax.ShapeDtypeStruct((tokens, width // GROUPS), F32)
    for group in range(GROUPS):
        parts += pl.pallas_call(
            functools.partial(inner_kernel, factor, group * HEADS // GROUPS),
            in_specs=[whole] * 4,
            out_specs=[whole] * 4,
            out_shape=[part_shape] * 4,
            compiler_params=small,
            cost_estimate=pl.CostEstimate(
                flops=9 * size * tokens // GROUPS,
                bytes_accessed=24 * size // GROUPS,
                transcendentals=0,
            ),
        )(*share_arrays, *rest_arrays)
    outs = []
    ends = (
        (True, share, rest_arrays, share_sums),
        (False, rest, share_arrays, rest_sums),
    )
    for first, pieces, arrays, sums in ends:
        fixed = 2 + 4 * GROUPS + n + len(sums)
        outs = pl.pallas_call(
            functools.partial(outer_kernel, factor, GROUPS, n, tiles, first),
            in_specs=[whole] * fixed + [there] * len(outs),
            out_specs=[there] * 4,
            scratch_shapes=[array] * 2
            + [stack, pltpu.SemaphoreType.DMA((2, tiles, HEADS // WRITE))],
            out_shape=[jax.ShapeDtypeStruct((tokens, width), BF16)] * 4,
            input_output_aliases={fixed + i: i for i in range(len(outs))},
            compiler_params=pltpu.CompilerParams(vmem_limit_bytes=8 * 2**20),
            cost_estimate=pl.CostEstimate(
                flops=4 * size * HEAD, bytes_accessed=16 * size, transcendentals=0
            ),
        )(*arrays, *parts, *pieces, *sums, *outs)
    return tuple(x.reshape(1, tokens, width) for x in outs)


def solution(mesh):
    n = mesh.shape["seq"]
    spec = P("resp", "seq", None)

    def body(*args):
        return per_device(n, mesh.shape["resp"], *args)

    return jax.shard_map(
        body,
        mesh=mesh,
        in_specs=(spec, spec, spec, spec, P()),
        out_specs=(spec, spec, spec, spec),
        check_vma=False,
    )
```

```python
import functools
import math

import jax
import jax.numpy as jnp
from jax import lax
from jax.experimental import pallas as pl
from jax.experimental.pallas import tpu as pltpu
from jax.sharding import PartitionSpec as P


HEADS = 8
HEAD = 128
TILE = 256
GROUPS = 4
STATE_VMEM = 8
WRITE = 4
F32 = jnp.float32
BF16 = jnp.bfloat16
AXES = ("seq", "resp")

NN = (((1,), (0,)), ((), ()))
NT = (((1,), (1,)), ((), ()))
TN = (((0,), (0,)), ((), ()))


def dot(a, b, dims):
    return lax.dot_general(a, b, dims, preferred_element_type=F32)


def kept(lengths_ref):
    row = lax.axis_index("resp")
    limit = lengths_ref[jnp.maximum(row - 1, 0)]
    return jnp.logical_or(row == 0, lax.axis_index("seq") < limit)


def tile_sums(tiles, keys_values, held, sums, total, ready):
    heads = [pl.ds(h * HEAD, HEAD) for h in range(HEADS)]
    for i in range(tiles):
        c = pl.ds(i * TILE, TILE)
        ready(i)
        for h in heads:
            new = dot(held[0][c, h], held[1][c, h], TN)
            if i < tiles - 1:
                sums[i][h, :] = new
                continue
            parts = [ref[h, :] for ref in sums] + [new]
            whole = sum(parts[1:], parts[0])
            upto = None
            for ref, part in zip(sums, parts):
                upto = part if upto is None else upto + part
                ref[h, :] = jnp.where(keys_values, upto, whole - upto if tiles > 2 else new)
            total[h, :] = whole


def cut_pieces(total, piece_refs):
    piece = piece_refs[0].shape[0]
    place = lax.axis_index("seq")
    for m, ref in enumerate(piece_refs):
        at = pl.multiple_of(jnp.bitwise_xor(place, m) * piece, piece)
        ref[...] = total[pl.ds(at, piece), :]


def share_kernel(n, tiles, lengths_hbm, *refs):
    prompt = lax.axis_index("resp") == 0
    sources = refs[:4]
    piece_refs = refs[4 : 4 + n]
    held = refs[4 + n : 8 + n]
    sums = refs[8 + n : 7 + n + tiles]
    total, lengths_ref, sem, count_sem = refs[-4:]
    counts = pltpu.make_async_copy(lengths_hbm, lengths_ref, count_sem)
    cut = [pl.ds(i * TILE, TILE) for i in range(tiles)]

    def copies(order):
        return [
            [pltpu.make_async_copy(sources[s].at[c], held[x].at[c], sem.at[x, i]) for x, s in part]
            for part in (tuple(enumerate(order))[:2], tuple(enumerate(order))[2:])
            for i, c in enumerate(cut)
        ]

    def start(order):
        for tile in copies(order):
            for copy in tile:
                copy.start()

    counts.start()

    @pl.when(prompt)
    def _():
        start((0, 1, 2, 3))

    @pl.when(jnp.logical_not(prompt))
    def _():
        start((2, 3, 0, 1))

    waits = copies((0, 1, 2, 3))
    counts.wait()

    def ready(at):
        for copy in waits[at]:
            copy.wait()
        pair = held[:2] if at < tiles else held[2:]

        @pl.when(jnp.logical_not(kept(lengths_ref)))
        def _():
            for ref in pair:
                ref[cut[at % tiles], :] = jnp.zeros((TILE, ref.shape[1]), BF16)

    tile_sums(tiles, prompt, held[:2], sums, total, ready)
    cut_pieces(total, piece_refs)
    for i in range(tiles):
        ready(tiles + i)


def rest_kernel(n, tiles, *refs):
    answers = lax.axis_index("resp") > 0
    sums = refs[2 + n : 1 + n + tiles]
    tile_sums(tiles, answers, refs[:2], sums, refs[-1], lambda i: None)
    cut_pieces(refs[-1], refs[2 : 2 + n])


def inner_kernel(factor, first, *refs):
    outs = refs[4:]
    rows = lax.broadcasted_iota(jnp.int32, (TILE, TILE), 0)
    columns = lax.broadcasted_iota(jnp.int32, (TILE, TILE), 1)
    causal = rows >= columns

    def write(arrays):
        for h in range(outs[0].shape[1] // HEAD):
            here = pl.ds((first + h) * HEAD, HEAD)
            there = pl.ds(h * HEAD, HEAD)
            for i in range(arrays[0].shape[0] // TILE):
                c = pl.ds(i * TILE, TILE)
                q, k, v, g = (ref[c, here] for ref in arrays)
                a = jnp.where(causal, dot(q, k, NT) * factor, 0.0).astype(BF16)
                p = jnp.where(causal, dot(g, v, NT) * factor, 0.0).astype(BF16)
                outs[0][c, there] = dot(a, v, NN)
                outs[1][c, there] = dot(p, k, NN)
                outs[2][c, there] = dot(p, q, TN)
                outs[3][c, there] = dot(a, g, TN)

    prompt = lax.axis_index("resp") == 0
    a, b, c, d = refs[:4]

    @pl.when(prompt)
    def _():
        write((c, a, b, d))

    @pl.when(jnp.logical_not(prompt))
    def _():
        write((a, c, d, b))


def outer_kernel(factor, groups, n, tiles, first, *refs):
    arrays = refs[:2]
    parts = refs[2 : 2 + 4 * groups]
    refs = refs[2 + 4 * groups :]
    pieces = refs[:n]
    sums = refs[n : n + tiles - 1]
    refs = refs[n + tiles - 1 :]
    outs = refs[:4] if first else refs[4:8]
    buffers = refs[-4:-2]
    state, sem = refs[-2:]
    place = lax.axis_index("seq")
    prompt = lax.axis_index("resp") == 0
    piece = pieces[0].shape[0]
    for m in range(n):
        at = pl.multiple_of(jnp.bitwise_xor(place, m) * piece, piece)
        state[pl.ds(at, piece), :] = pieces[m][...]
    span = HEADS // groups

    def write(sides, added):
        copies = []
        for tile in range(tiles):
            c = pl.ds(tile * TILE, TILE)
            for head in range(HEADS):
                h = pl.ds(head * HEAD, HEAD)
                within = pl.ds(head % span * HEAD, HEAD)
                total = state[h, :]
                if added[tile] is not None:
                    total = total + added[tile][h, :]
                low = total.astype(BF16)
                for buffer, (which, source, dims) in zip(buffers, sides):
                    part = parts[head // span * 4 + which][c, within]
                    out = part + factor * dot(arrays[source][c, h], low, dims)
                    buffer[c, h] = out.astype(BF16)
                if head % WRITE == WRITE - 1:
                    at = head // WRITE
                    wide = pl.ds(at * WRITE * HEAD, WRITE * HEAD)
                    for i, (which, _, _) in enumerate(sides):
                        copy = pltpu.make_async_copy(
                            buffers[i].at[c, wide], outs[which].at[c, wide], sem.at[i, tile, at]
                        )
                        copy.start()
                        copies.append(copy)
        for copy in copies:
            copy.wait()

    @pl.when(prompt == first)
    def _():
        write(((0, 0, NN), (1, 1, NT)), (None, *sums))

    @pl.when(prompt != first)
    def _():
        write(((2, 1, NT), (3, 0, NN)), (*sums, None))


def pair_kernel(mine_ref, new_ref, send_ref, sum_ref):
    row = lax.axis_index("resp")
    mine = mine_ref[...]
    new = new_ref[...]
    both = mine + new
    send_ref[...] = jnp.where(row == 0, mine, jnp.where(row == 1, new, both))
    sum_ref[...] = jnp.where(row == 0, new, mine)


def level_kernel(layers, send_ref, sum_ref, *refs):
    row = lax.axis_index("resp")
    layer = lax.div(row, 2)
    answer = sum_ref[...]
    prompt = jnp.zeros_like(answer)
    for k in range(1, layers):
        new = refs[k - 1][...]
        answer = answer + new
        prompt = prompt + jnp.where(layer == k, new, 0.0)
    total = jnp.where(layer == 0, answer, prompt)
    send = send_ref[...]
    own_ref, give_ref = refs[-2:]
    own_ref[...] = jnp.where(row == 1, send, total)
    give_ref[...] = jnp.where(row == 0, send, total)


def scan_kernel(n, first, *refs):
    place = lax.axis_index("seq")
    row = lax.axis_index("resp")
    prompt = row == 0
    count = n if first else n + 2
    came = refs[:count]
    outs = refs[count : count + n]
    order, sums = refs[-2:]
    for m in range(n):
        order[jnp.bitwise_xor(place, m)] = came[m][...]
    core = lax.rem(row, 2)
    half = came[-1].shape[0] if not first else refs[count + n].shape[0]
    here = pl.ds(pl.multiple_of(core * half, half), half)
    there = pl.ds(pl.multiple_of((1 - core) * half, half), half)
    if first:
        forward = prompt
        before = jnp.zeros(order.shape[1:], F32)
    else:
        forward = jnp.logical_not(prompt)
        sums[0, here, :] = came[n][...]
        sums[0, there, :] = came[n + 1][...]
        before = sums[0]
    after = before
    for s in range(n):
        sums[s] = before
        before = before + order[s]
    for s in reversed(range(n)):
        sums[s] = jnp.where(forward, sums[s], after)
        after = after + order[s]
    for m in range(n):
        outs[m][...] = sums[jnp.bitwise_xor(place, m)]
    if first:
        order[0] = before
        refs[count + n][...] = order[0, here, :]
        refs[count + n + 1][...] = order[0, there, :]


def per_device(n, rows, queries, keys, values, grad_out, lengths):
    tokens = queries.shape[1]
    width = queries.shape[2]
    factor = 1.0 / math.sqrt(2.0 * tokens * n)
    q, k, v, g = (x.reshape(tokens, width) for x in (queries, keys, values, grad_out))
    whole = pl.BlockSpec(memory_space=pltpu.VMEM)
    size = tokens * width

    def line(s, r):
        return s * rows + r

    def move(x, pairs):
        return lax.ppermute(x, AXES, pairs)

    there = pl.BlockSpec(memory_space=pltpu.HBM)
    array = pltpu.VMEM((tokens, width), BF16)
    stack = pltpu.VMEM((HEADS * HEAD, HEAD), F32)
    counts = pltpu.SMEM(lengths.shape, jnp.int32)
    tiles = tokens // TILE
    piece = HEADS * HEAD // n
    piece_shape = jax.ShapeDtypeStruct((piece, HEAD), F32)
    half_shape = jax.ShapeDtypeStruct((piece // 2, HEAD), F32)
    small = pltpu.CompilerParams(vmem_limit_bytes=6 * 2**20)

    def far(x):
        return pltpu.with_memory_space_constraint(x, pltpu.HBM)

    array_shape = jax.ShapeDtypeStruct((tokens, width), BF16)
    sums_shape = [jax.ShapeDtypeStruct((HEADS * HEAD, HEAD), F32)] * (tiles - 1)
    grant = pltpu.CompilerParams(vmem_limit_bytes=STATE_VMEM * 2**20)
    work = pl.CostEstimate(flops=2 * size * HEAD, bytes_accessed=4 * size, transcendentals=0)
    made = pl.pallas_call(
        functools.partial(share_kernel, n, tiles),
        in_specs=[there] * 5,
        out_specs=[whole] * (n + 3 + tiles),
        scratch_shapes=[
            stack,
            counts,
            pltpu.SemaphoreType.DMA((4, tiles)),
            pltpu.SemaphoreType.DMA,
        ],
        out_shape=[piece_shape] * n + [array_shape] * 4 + sums_shape,
        compiler_params=grant,
        cost_estimate=work,
    )(far(lengths), far(k), far(v), far(q), far(g))
    share, share_sums = made[:n], made[n + 4 :]
    share_arrays, rest_arrays = made[n : n + 2], made[n + 2 : n + 4]
    made = pl.pallas_call(
        functools.partial(rest_kernel, n, tiles),
        in_specs=[whole] * 2,
        out_specs=[whole] * (n - 1 + tiles),
        scratch_shapes=[stack],
        out_shape=[piece_shape] * n + sums_shape,
        compiler_params=grant,
        cost_estimate=work,
    )(*rest_arrays)
    rest, rest_sums = made[:n], made[n:]

    def swapped(pieces):
        came = [pieces[0]]
        for m in range(1, n):
            came.append(
                move(
                    pieces[m],
                    [(line(s, r), line(s ^ m, r)) for s in range(n) for r in range(rows)],
                )
            )
        return came

    def scan(first, *pieces):
        shapes = [piece_shape] * n + [half_shape] * (2 * first)
        return pl.pallas_call(
            functools.partial(scan_kernel, n, first),
            in_specs=[whole] * len(pieces),
            out_specs=[whole] * len(shapes),
            out_shape=shapes,
            scratch_shapes=[pltpu.VMEM((n, piece, HEAD), F32)] * 2,
            compiler_params=small,
        )(*pieces)

    *share, mine, give = scan(True, *swapped(share))
    rest = swapped(rest)
    share = swapped(share)

    def across(x, bits):
        return move(x, [(line(s, r), line(s, r ^ bits)) for s in range(n) for r in range(rows)])

    def combine(kernel, *inputs):
        return pl.pallas_call(
            kernel,
            in_specs=[whole] * len(inputs),
            out_specs=[whole] * 2,
            out_shape=[half_shape] * 2,
            compiler_params=small,
        )(*inputs)

    layers = rows // 2
    send, gathered = combine(pair_kernel, mine, across(give, 1))
    levels = []
    for z in range(1, layers):
        meets = {0: z, z: 0}
        pairs = [
            (line(s, r), line(s, 2 * meets[r // 2] + r % 2 if r // 2 in meets else r ^ 1))
            for s in range(n)
            for r in range(rows)
        ]
        levels.append(move(send, pairs))
    own, give = combine(functools.partial(level_kernel, layers), send, gathered, *levels)
    new = across(give, 1)
    rest = swapped(scan(False, *rest, own, new))
    parts = []
    part_shape = jax.ShapeDtypeStruct((tokens, width // GROUPS), F32)
    for group in range(GROUPS):
        parts += pl.pallas_call(
            functools.partial(inner_kernel, factor, group * HEADS // GROUPS),
            in_specs=[whole] * 4,
            out_specs=[whole] * 4,
            out_shape=[part_shape] * 4,
            compiler_params=small,
            cost_estimate=pl.CostEstimate(
                flops=9 * size * tokens // GROUPS,
                bytes_accessed=24 * size // GROUPS,
                transcendentals=0,
            ),
        )(*share_arrays, *rest_arrays)
    outs = []
    ends = (
        (True, share, rest_arrays, share_sums),
        (False, rest, share_arrays, rest_sums),
    )
    for first, pieces, arrays, sums in ends:
        fixed = 2 + 4 * GROUPS + n + len(sums)
        outs = pl.pallas_call(
            functools.partial(outer_kernel, factor, GROUPS, n, tiles, first),
            in_specs=[whole] * fixed + [there] * len(outs),
            out_specs=[there] * 4,
            scratch_shapes=[array] * 2
            + [stack, pltpu.SemaphoreType.DMA((2, tiles, HEADS // WRITE))],
            out_shape=[jax.ShapeDtypeStruct((tokens, width), BF16)] * 4,
            input_output_aliases={fixed + i: i for i in range(len(outs))},
            compiler_params=pltpu.CompilerParams(vmem_limit_bytes=8 * 2**20),
            cost_estimate=pl.CostEstimate(
                flops=4 * size * HEAD, bytes_accessed=16 * size, transcendentals=0
            ),
        )(*arrays, *parts, *pieces, *sums, *outs)
    return tuple(x.reshape(1, tokens, width) for x in outs)


def solution(mesh):
    n = mesh.shape["seq"]
    spec = P("resp", "seq", None)

    def body(*args):
        return per_device(n, mesh.shape["resp"], *args)

    return jax.shard_map(
        body,
        mesh=mesh,
        in_specs=(spec, spec, spec, spec, P()),
        out_specs=(spec, spec, spec, spec),
        check_vma=False,
    )
```
